512 devices in a mesh: lon: 64 (over z_hi, x, y), ch: 8 (over z_lo, core).
Axes of the slice: x: 4, y: 8, z: 8 (z_hi: 2, z_lo: 4; z = z_hi * 4 + z_lo), core: 2. Of those that a mesh axis runs over, the one named last changes fastest.
Arguments:
- coarse: bfloat16 [16, 4, 256, 1024], P(None, None, 'lon', 'ch'), may hold values from -6 to 6
- up_kernel: bfloat16 [4, 4, 1024, 512], P(None, None, 'ch', 'lon'), may hold values from -0.09375 to 0.09375
- up_bias: float32 [512], replicated, may hold values from -3 to 3
- conv_kernel: bfloat16 [3, 3, 512, 512], P(None, None, 'lon'), may hold values from -0.09375 to 0.09375
- conv_bias: float32 [512], replicated, may hold values from -3 to 3
Outputs:
- fine_out: bfloat16 [32, 4, 512, 512], P('ch', None, 'lon')
The draws below stay inside these ranges and needn't reach their ends.
All inputs are finite; a program needn't handle non-finite values.
Results may differ from the reference program's by a relative error of at most 0.015.
Values may be sent and summed in bfloat16 or wider, within the bound.
A program may use at most 64 MiB of HBM per device.

```python
import jax
import jax.numpy as jnp
from jax import lax

CIN = 1024
COUT = 512
BATCH = 4
LAT = 16
LONC = 256
LATF = 32
LONF = 512
N_CH = 8


def steps_of(own_key, extent, split, low, largest):
    loudness, own = 1.0, jax.random.fold_in(own_key, 6)
    for dim, blocks in split:
        draws = jnp.exp(jax.random.uniform(jax.random.fold_in(own, dim), (blocks,), jnp.float32, low / len(split), largest / len(split)))
        loudness = loudness * jnp.repeat(draws, extent[dim] // blocks).reshape([-1 if axis == dim else 1 for axis in range(len(extent))])
    return loudness


def centred(rng, extent, deviation, bound, cuts=(), dtype=jnp.bfloat16):
    level = steps_of(rng, extent, cuts, -0.22, 0.18) if cuts else 1.0
    array = jax.random.normal(rng, extent, jnp.float32) * deviation * level
    return jnp.minimum(jnp.maximum(array, -bound), bound).astype(dtype)


def setup_inputs(seed: int = 0) -> dict:
    key_of = jax.random.split(jax.random.key(seed), 6)
    return {
        "coarse": centred(key_of[0], (LAT, BATCH, LONC, CIN), 1.0, 6.0, ((2, 64), (3, 8))),
        "up_kernel": centred(key_of[1], (4, 4, CIN, COUT), (4 * CIN) ** -0.5, 0.09375, ((2, 8), (3, 64))),
        "up_bias": centred(key_of[2], (COUT,), 0.5, 3.0, (), jnp.float32),
        "conv_kernel": centred(key_of[3], (3, 3, COUT, COUT), (9 * COUT) ** -0.5, 0.09375, ((2, 64),)),
        "conv_bias": centred(key_of[4], (COUT,), 0.5, 3.0, (), jnp.float32),
    }


TAPS = (((1, 1), (3, 0)), ((2, 1), (0, 2)))


def tap_dot(piece, weight):
    flat = piece.reshape(-1, piece.shape[-1])
    result = jnp.dot(flat, weight, preferred_element_type=jnp.float32)
    return result.reshape(piece.shape[:-1] + (weight.shape[-1],))


def upsample(padded, lon_count, weights):
    rows = padded.shape[0] - 2
    batch = padded.shape[1]
    phases = []
    for p in range(2):
        columns = []
        for q in range(2):
            total = None
            for a, row_off in TAPS[p]:
                for c, col_off in TAPS[q]:
                    piece = padded[row_off:row_off + rows, :, col_off:col_off + lon_count, :]
                    term = tap_dot(piece, weights[a, c])
                    total = term if total is None else total + term
            columns.append(total)
        phases.append(jnp.stack(columns, axis=3))
    stacked = jnp.stack(phases, axis=1)
    return stacked.reshape(2 * rows, batch, 2 * lon_count, weights.shape[-1])


def reference(coarse, up_kernel, up_bias, conv_kernel, conv_bias):
    block = CIN // N_CH

    def add_block(k, total):
        start = (k * block).astype(jnp.int32)
        piece = lax.dynamic_slice_in_dim(coarse, start, block, 3)
        kernel = lax.dynamic_slice_in_dim(up_kernel, start, block, 2)
        padded = jnp.pad(piece, ((1, 1), (0, 0), (0, 0), (0, 0)))
        padded = jnp.concatenate([padded[:, :, -1:], padded, padded[:, :, :1]], axis=2)
        partial_value = upsample(padded, LONC, kernel).astype(jnp.bfloat16)
        return total + partial_value.astype(jnp.float32)

    total = jnp.zeros((LATF, BATCH, LONF, COUT), jnp.float32)
    total = lax.fori_loop(0, N_CH, add_block, total)
    hidden = jax.nn.gelu(total + up_bias, approximate=False).astype(jnp.bfloat16)
    padded = jnp.pad(hidden, ((1, 1), (0, 0), (0, 0), (0, 0)))
    padded = jnp.concatenate([padded[:, :, -1:], padded, padded[:, :, :1]], axis=2)
    result = jnp.zeros((LATF, BATCH, LONF, COUT), jnp.float32) + conv_bias
    for d in range(3):
        for t in range(3):
            result = result + tap_dot(padded[d:d + LATF, :, t:t + LONF, :], conv_kernel[d, t])
    return result.astype(jnp.bfloat16)
```

```python
import jax
import jax.numpy as jnp
from jax import lax
from jax.experimental import pallas as pl
from jax.experimental.pallas import tpu as pltpu
from jax.sharding import PartitionSpec as P

MESH = pl.DeviceIdType.MESH
F32, BF16 = jnp.float32, jnp.bfloat16
NX, NY = 4, 8
TAPS = (((1, 1), (3, 0)), ((2, 1), (0, 2)))
PHASES = ((0, 0), (0, 1), (1, 0), (1, 1))
N_SEM = 256


def grid_of(rows, cols):
    return (
        lax.broadcasted_iota(jnp.int32, (rows, cols), 0),
        lax.broadcasted_iota(jnp.int32, (rows, cols), 1),
    )


def pick(mask):
    return jnp.where(mask, 1.0, 0.0).astype(BF16)


def dot(a, b):
    return jnp.dot(a, b, preferred_element_type=F32)


def dot_t(a, b):
    return lax.dot_general(a, b, (((1,), (1,)), ((), ())), preferred_element_type=F32)


def kernel(
    coarse, upk, upb, ck, cb, out,
    uw, cw, ce, nbo, ne, act, part, recv, hid, es, er, g,
    send_sem, recv_sem, local_sem,
):
    lon = lax.axis_index("lon")
    k = lax.axis_index("ch")
    zh, x, y = lon // 32, lax.rem(lon // 8, 4), lax.rem(lon, 8)
    zl, c = k // 2, lax.rem(k, 2)
    other = 1 - zh
    sib = k + 1 - 2 * c
    left, right = lax.rem(lon + 63, 64), lax.rem(lon + 1, 64)

    def dev(xx, yy, plane=None):
        return {"lon": (zh if plane is None else plane) * 32 + xx * 8 + yy, "ch": k}

    def at(l, kk):
        return {"lon": l, "ch": kk}

    def ring(v, d, n):
        return lax.rem(v + (d % n), n)

    sibling = at(lon, sib)

    barrier = pltpu.get_barrier_semaphore()

    def greet(device):
        pl.semaphore_signal(barrier, inc=1, device_id=device, device_id_type=MESH)

    for d in range(1, NX):
        greet(dev(ring(x, d, NX), y))
    for d in range(1, NY):
        greet(dev(x, ring(y, d, NY)))
    greet(dev(x, y, other))
    for d in range(1, 4):
        greet(at(lon, ring(zl, d, 4) * 2 + c))
    for side in (left, right):
        greet(at(side, k))

    @pl.when(k > 0)
    def _():
        for l in (left, lon, right):
            greet(at(l, k - 1))

    @pl.when(k < 7)
    def _():
        for l in (left, lon, right):
            greet(at(l, k + 1))

    pl.semaphore_wait(barrier, 16 + 3 * ((k + 7) // 8) + 3 * ((14 - k) // 8))

    state = {"sem": 0, "local": 0}
    sends = []

    def describe(src, dst, device, index=None):
        if index is None:
            index = state["sem"]
            state["sem"] += 1
        return pltpu.make_async_remote_copy(
            src_ref=src, dst_ref=dst, send_sem=send_sem.at[index], recv_sem=recv_sem.at[index],
            device_id=device, device_id_type=MESH,
        )

    def send(src, dst, device):
        copy = describe(src, dst, device)
        copy.start()
        sends.append(copy)
        return copy

    def local(src, dst):
        copy = pltpu.make_async_copy(src, dst, local_sem.at[state["local"]])
        state["local"] += 1
        copy.start()
        return copy

    class Gather:
        def __init__(self, ref, lanes, source, taps_a, taps_b, start):
            self.ref, self.lanes, self.source = ref, lanes, source
            self.a, self.b, self.t = taps_a, taps_b, start
            self.mirrors = []
            block = self.block(zh, x, y, pl.ds(0, taps_a.size + taps_b.size))
            self.own = local(source, block)
            self.z = send(source, block, dev(x, y, other))
            self.own_done = False

        def block(self, plane, xx, yy, taps):
            return self.ref.at[taps, plane * 4 + xx, pl.ds(pl.multiple_of(yy * 8, 8), 8), self.lanes]

        def by_x(self, plane, xx):
            return self.ref.at[self.b, plane * 4 + xx, :, self.lanes]

        def by_y(self, plane, yy):
            return self.ref.at[
                self.a, pl.ds(plane * 4, 4), pl.ds(pl.multiple_of(yy * 8, 8), 8), self.lanes
            ]

        def mirror(self, unit):
            self.mirrors.append(send(unit, unit, sibling))

        def first(self, plane, far, taps, count, coordinate, device):
            block = self.block(plane, x, y, taps)
            source = block if far else self.source.at[taps]
            return [send(source, block, device(ring(coordinate, d, count))) for d in range(1, count)]

        def settle(self, far):
            if not far and not self.own_done:
                self.own.wait()
                self.own_done = True

        def arrive(self, far):
            if far and self.z is not None:
                self.z.wait_recv()
                self.z = None

        def chain_b(self, far):
            plane = other if far else zh
            t = self.t + (4.2 if far else 0.0)
            if far:
                yield t
                self.arrive(far)
            copies = self.first(plane, far, self.b, NY, y, lambda yy: dev(x, yy))
            yield t + 4.0
            for copy in copies:
                copy.wait_recv()
            self.settle(far)
            unit = self.by_x(plane, x)
            to_right = send(unit, unit, dev(ring(x, 1, NX), y))
            to_left = send(unit, unit, dev(ring(x, -1, NX), y))
            self.mirror(unit)
            yield t + 7.0
            to_right.wait_recv()
            to_left.wait_recv()
            from_left, from_right = self.by_x(plane, ring(x, -1, NX)), self.by_x(plane, ring(x, 1, NX))
            if far:
                forward = send(from_right, from_right, dev(ring(x, -1, NX), y))
            else:
                forward = send(from_left, from_left, dev(ring(x, 1, NX), y))
            self.mirror(from_left)
            self.mirror(from_right)
            yield t + 10.0
            forward.wait_recv()
            self.mirror(self.by_x(plane, ring(x, 2, NX)))

        def chain_a(self, far):
            plane = other if far else zh
            t = self.t + (4.2 if far else 0.0)
            if far:
                yield t
                self.arrive(far)
            copies = self.first(plane, far, self.a, NX, x, lambda xx: dev(xx, y))
            yield t + 2.5
            for copy in copies:
                copy.wait_recv()
            self.settle(far)
            unit = self.by_y(plane, y)
            up = send(unit, unit, dev(x, ring(y, 1, NY)))
            down = send(unit, unit, dev(x, ring(y, -1, NY)))
            self.mirror(unit)
            ups, downs = (3, 4) if far else (4, 3)
            for step in range(1, 5):
                yield t + 2.5 + 2.0 * step
                if step <= ups:
                    up.wait_recv()
                    unit = self.by_y(plane, ring(y, -step, NY))
                    if step < ups:
                        up = send(unit, unit, dev(x, ring(y, 1, NY)))
                    self.mirror(unit)
                if step <= downs:
                    down.wait_recv()
                    unit = self.by_y(plane, ring(y, step, NY))
                    if step < downs:
                        down = send(unit, unit, dev(x, ring(y, -1, NY)))
                    self.mirror(unit)

        def chains(self):
            made = []
            for far in (False, True):
                if self.b.size:
                    made.append(self.chain_b(far))
                if self.a.size:
                    made.append(self.chain_a(far))
            return made

        def finish(self):
            for copy in self.mirrors:
                copy.wait_recv()

    def run(chains):
        waiting = []
        for order, chain in enumerate(chains):
            step = next(chain, None)
            if step is not None:
                waiting.append((step, order, chain))
        while waiting:
            waiting.sort(key=lambda item: item[:2])
            _, order, chain = waiting.pop(0)
            step = next(chain, None)
            if step is not None:
                waiting.append((step, order, chain))

    c128, c256 = pl.multiple_of(c * 128, 128), pl.multiple_of(c * 256, 256)
    up_gather = Gather(uw, pl.ds(c128, 128), upk, pl.ds(0, 6), pl.ds(6, 10), 0.0)
    up_chains = up_gather.chains()
    firsts = [chain for chain in up_chains]

    block = coarse[...].reshape(256, 128)
    m, n = grid_of(64, 256)
    ce[0] = dot(pick(n == 4 * m), block).astype(BF16)
    ce[1] = dot(pick(n == 4 * m + 3), block).astype(BF16)
    arrivals = [send(coarse, nbo, sibling)]

    def beside(kk):
        return [
            send(ce.at[1], ne.at[c, 0], at(right, kk)),
            send(ce.at[0], ne.at[c, 1], at(left, kk)),
        ]

    arrivals += beside(k) + beside(sib)

    def act_chain():
        yield 3.9
        for copy in arrivals:
            copy.wait_recv()
        act[:, pl.ds(0, 1)] = jnp.zeros((3, 1, 16, 256), BF16)
        act[:, pl.ds(17, 1)] = jnp.zeros((3, 1, 16, 256), BF16)
        row, col = grid_of(256, 256)
        low = pick((col == row - 1) & ((row & 3) != 0))
        high = pick((col == row + 1) & ((row & 3) != 3))
        row, col = grid_of(256, 64)
        low_edge, high_edge = pick(row == 4 * col), pick(row == 4 * col + 3)
        for mine in (True, False):
            parity = c if mine else 1 - c
            lanes = pl.ds(pl.multiple_of(parity * 128, 128), 128)
            here = block if mine else nbo[...].reshape(256, 128)
            before = dot(low, here) + dot(low_edge, ne[parity, 0])
            after = dot(high, here) + dot(high_edge, ne[parity, 1])
            act[0, pl.ds(1, 16), :, lanes] = before.astype(BF16).reshape(16, 16, 128)
            act[1, pl.ds(1, 16), :, lanes] = here.reshape(16, 16, 128)
            act[2, pl.ds(1, 16), :, lanes] = after.astype(BF16).reshape(16, 16, 128)

    run(firsts + [act_chain()])
    conv_gather = Gather(cw, pl.ds(c256, 256), ck.at[:, :, pl.ds(c256, 256)], pl.ds(0, 4), pl.ds(4, 5), 20.0)
    conv_chains = conv_gather.chains()
    up_gather.finish()

    scatters = []
    for phase, (p, q) in enumerate(PHASES):
        total = None
        for a, row_off in TAPS[p]:
            for t, col_off in TAPS[q]:
                piece = jnp.concatenate(
                    [act[col_off, pl.ds(4 * band + 2 * c + row_off, 2)].reshape(32, 256) for band in range(4)],
                    axis=0,
                )
                term = dot_t(piece, uw[4 * a + t].reshape(512, 256))
                total = term if total is None else total + term
        part[:, phase] = total.astype(BF16).reshape(4, 2, 16, 512)
        for d in range(1, 4):
            target = ring(zl, d, 4)
            scatters.append(send(part.at[target, phase], recv.at[zl, phase], at(lon, target * 2 + c)))

    def mid_chain():
        yield 26.0
        for phase, (p, q) in enumerate(PHASES):
            total = part[zl, phase].astype(F32)
            for d in range(1, 4):
                scatters[3 * phase + d - 1].wait_recv()
                total = total + recv[ring(zl, -d, 4), phase].astype(F32)
            v = total + upb[...].reshape(1, 1, 512)
            h = (0.5 * v * (1.0 + lax.erf(v * (0.5**0.5)))).astype(BF16)
            hid[q, 1 + p] = h[0]
            hid[q, 3 + p] = h[1]
        m, n = grid_of(32, 64)
        wanted = 4 * (4 * (m >> 3) + (m & 7))
        real = (m & 7) < 4
        es[0] = dot(pick((n == wanted) & real), hid[0, pl.ds(1, 4)].reshape(64, 512)).astype(BF16).reshape(4, 8, 512)
        es[1] = dot(pick((n == wanted + 3) & real), hid[1, pl.ds(1, 4)].reshape(64, 512)).astype(BF16).reshape(4, 8, 512)
        edges = [
            send(es.at[1], er.at[0, pl.ds(1, 4)], at(right, k)),
            send(es.at[0], er.at[1, pl.ds(1, 4)], at(left, k)),
        ]
        first = state["sem"]
        state["sem"] += 6
        upward = lambda: [
            describe(hid.at[:, pl.ds(4, 1)], hid.at[:, pl.ds(0, 1)], at(lon, k + 1), first),
            describe(es.at[1, pl.ds(3, 1)], er.at[0, pl.ds(0, 1)], at(right, k + 1), first + 1),
            describe(es.at[0, pl.ds(3, 1)], er.at[1, pl.ds(0, 1)], at(left, k + 1), first + 2),
        ]
        downward = lambda: [
            describe(hid.at[:, pl.ds(1, 1)], hid.at[:, pl.ds(5, 1)], at(lon, k - 1), first + 3),
            describe(es.at[1, pl.ds(0, 1)], er.at[0, pl.ds(5, 1)], at(right, k - 1), first + 4),
            describe(es.at[0, pl.ds(0, 1)], er.at[1, pl.ds(5, 1)], at(left, k - 1), first + 5),
        ]

        @pl.when(k < 7)
        def _():
            for copy in upward():
                copy.start()

        @pl.when(k > 0)
        def _():
            for copy in downward():
                copy.start()

        yield 30.0
        for copy in edges:
            copy.wait_recv()

        @pl.when(k > 0)
        def _():
            for copy in upward():
                copy.wait_recv()

        @pl.when(k < 7)
        def _():
            for copy in downward():
                copy.wait_recv()

        @pl.when(k < 7)
        def _():
            for copy in upward():
                copy.wait_send()

        @pl.when(k > 0)
        def _():
            for copy in downward():
                copy.wait_send()

        @pl.when(k == 0)
        def _():
            hid[:, pl.ds(0, 1)] = jnp.zeros((2, 1, 16, 512), BF16)
            er[:, pl.ds(0, 1)] = jnp.zeros((2, 1, 8, 512), BF16)

        @pl.when(k == 7)
        def _():
            hid[:, pl.ds(5, 1)] = jnp.zeros((2, 1, 16, 512), BF16)
            er[:, pl.ds(5, 1)] = jnp.zeros((2, 1, 8, 512), BF16)

        even, odd = hid[0].reshape(96, 512), hid[1].reshape(96, 512)
        row, col = grid_of(96, 96)
        low = pick((col == row - 1) & ((row & 3) != 0))
        high = pick((col == row + 1) & ((row & 3) != 3))
        row, col = grid_of(96, 48)
        place = 8 * (row >> 4) + ((row >> 2) & 3)
        low_edge = pick((col == place) & ((row & 3) == 0))
        high_edge = pick((col == place) & ((row & 3) == 3))
        before = dot(low, odd) + dot(low_edge, er[0].reshape(48, 512))
        after = dot(high, even) + dot(high_edge, er[1].reshape(48, 512))
        g[0, :, 0] = before.astype(BF16).reshape(6, 16, 512)
        g[0, :, 1] = hid[0]
        g[1, :, 0] = hid[0]
        g[1, :, 1] = hid[1]
        g[2, :, 0] = hid[1]
        g[2, :, 1] = after.astype(BF16).reshape(6, 16, 512)

    run(conv_chains + [mid_chain()])
    conv_gather.finish()

    total = None
    for d in range(3):
        for t in range(3):
            term = dot(g[t, pl.ds(d, 4)].reshape(128, 512), cw[3 * d + t].reshape(512, 512))
            total = term if total is None else total + term
    total = total + cb[...]
    out[...] = total.astype(BF16).reshape(4, 2, 16, 512)
    for copy in sends:
        copy.wait_send()


def shards(coarse, up_kernel, up_bias, conv_kernel, conv_bias):
    vmem = pl.BlockSpec(memory_space=pltpu.VMEM)
    result = pl.pallas_call(
        kernel,
        out_shape=jax.ShapeDtypeStruct((4, 2, 16, 512), BF16),
        in_specs=[vmem] * 5,
        out_specs=vmem,
        scratch_shapes=[
            pltpu.VMEM((16, 8, 64, 256), BF16),
            pltpu.VMEM((9, 8, 64, 512), BF16),
            pltpu.VMEM((2, 64, 128), BF16),
            pltpu.VMEM((16, 16, 128), BF16),
            pltpu.VMEM((2, 2, 64, 128), BF16),
            pltpu.VMEM((3, 18, 16, 256), BF16),
            pltpu.VMEM((4, 4, 2, 16, 512), BF16),
            pltpu.VMEM((4, 4, 2, 16, 512), BF16),
            pltpu.VMEM((2, 6, 16, 512), BF16),
            pltpu.VMEM((2, 4, 8, 512), BF16),
            pltpu.VMEM((2, 6, 8, 512), BF16),
            pltpu.VMEM((3, 6, 2, 16, 512), BF16),
            pltpu.SemaphoreType.DMA((N_SEM,)),
            pltpu.SemaphoreType.DMA((N_SEM,)),
            pltpu.SemaphoreType.DMA((2,)),
        ],
        compiler_params=pltpu.CompilerParams(collective_id=0, has_side_effects=True),
    )(
        coarse.reshape(16, 16, 128),
        up_kernel.transpose(0, 1, 3, 2).reshape(16, 8, 128),
        up_bias.reshape(1, 512),
        conv_kernel.reshape(9, 8, 512),
        conv_bias.reshape(1, 512),
    )
    return result.reshape(4, 2, 4, 4, 512).transpose(0, 2, 3, 1, 4).reshape(4, 4, 8, 512)


def solution(mesh):
    return jax.shard_map(
        shards,
        mesh=mesh,
        in_specs=(
            P(None, None, "lon", "ch"),
            P(None, None, "ch", "lon"),
            P(),
            P(None, None, "lon", None),
            P(),
        ),
        out_specs=P("ch", None, "lon", None),
        check_vma=False,
    )
```
